128 devices in a mesh: row: 8 (over x, core), blk: 16 (over z, y).
Axes of the slice: x: 4, y: 4, z: 4, core: 2. Of those that a mesh axis runs over, the one named last changes fastest.
Arguments:
- panel: float32 [256, 524288], P(None, ('row', 'blk'))
- logits: float32 [524288], P(('row', 'blk')), may hold values from -6 to 6
- signs: int32 [524288], P(('row', 'blk')), may hold values from -1 to 1, as said below
- samples: int32 [128, 96], P(('row', 'blk')), may hold values from 0 to 4095, as said below
- counts: int32 [128], P(('row', 'blk')), may hold values from 32 to 96, as said below
Outputs:
- conditioned: float32 [256, 524288], P(None, ('row', 'blk'))
The draws below stay inside these ranges and needn't reach their ends.
Inputs may be any that keep to these rules, and one draw needn't show every extreme that they name: `signs`: each entry is -1 or 1. Entry [e, s] names frequency e + 128 * samples[e, s]; an offset may repeat within a row. Row e of samples uses its first counts[e] slots; the others are ignored.
All inputs are finite; a program needn't handle non-finite values.
Results may differ from the reference program's by a relative error of at most 0.000052.
Values sent between devices are 32-bit elements; how exact they have to be, the bound alone decides.
No kernel may reach another device: no remote copies, remote signals or barrier semaphores. Data moves between devices by JAX's collectives and lax.ppermute only.
A program may use at most 128 MiB of HBM per device.

```python
import math
import jax
import jax.numpy as jnp
from jax import lax

P_SIZE = 256
SMAX = 96
ROWS_DEV = 4096
SHARDS = 128
ROWS = 524288


def draw_panel(key, part):
    base_key, column_key, row_key = jax.random.split(key, 3)
    column_scale = jnp.exp(jax.random.uniform(column_key, (P_SIZE, 1), jnp.float32, 0.0, math.log(10.0)))
    row_scale = jnp.exp(jax.random.uniform(row_key, (1, ROWS), jnp.float32, 0.0, math.log(10.0)))
    entries = jnp.clip(jax.random.normal(base_key, (P_SIZE, ROWS), jnp.float32), -4.0, 4.0)
    return (entries * column_scale * row_scale).astype(jnp.float32)


def draw_signs(key, part):
    coins = jax.random.randint(key, (ROWS,), 0, 2)
    return (2 * coins - 1).astype(jnp.int32)


def draw_samples(key, part):
    value_key, place_key = jax.random.split(key)
    slots = SHARDS * SMAX
    offsets = jax.random.randint(value_key, (slots,), 0, ROWS_DEV)
    position = jax.random.randint(place_key, (), 0, slots - 1)
    offsets = offsets.at[position].set(ROWS_DEV - 1)
    offsets = offsets.at[position + 1].set(0)
    return offsets.reshape(SHARDS, SMAX).astype(jnp.int32)


def draw_counts(key, part):
    device_index = jnp.arange(SHARDS, dtype=jnp.int32)
    lowest = SMAX // 3
    baseline = lowest + device_index * (SMAX - lowest) // (SHARDS - 1)
    jitter = jax.random.randint(key, (SHARDS,), 0, 9)
    inner = (device_index > 0) & (device_index < SHARDS - 1)
    result = jnp.minimum(SMAX, baseline + jnp.where(inner, jitter, 0))
    return result.astype(jnp.int32)


def level_of(stream_key, dims, cuts, smallest, largest):
    def one(dim, blocks):
        steps = jax.random.uniform(jax.random.fold_in(jax.random.fold_in(stream_key, 6), dim), (blocks,), jnp.float32, smallest / len(cuts), largest / len(cuts))
        return jnp.repeat(jnp.exp(steps), dims[dim] // blocks).reshape((-1,) + (1,) * (len(dims) - dim - 1))

    level = one(*cuts[0])
    for cut in cuts[1:]:
        level = level * one(*cut)
    return level


def scatter_about(key, extent, scale, limit, pieces=(), held_as=jnp.bfloat16):
    factor_of = level_of(key, extent, pieces, -0.22, 0.18) if pieces else 1.0
    drawn = jax.random.normal(key, extent, jnp.float32) * scale * factor_of
    return jnp.minimum(jnp.maximum(drawn, -limit), limit).astype(held_as)


def setup_inputs(seed: int = 0) -> dict:
    streams_of = jax.random.split(jax.random.key(seed), 6)
    panel = draw_panel(jax.random.fold_in(streams_of[5], 71), 0)
    logits = scatter_about(streams_of[1], (ROWS,), 2.0, 6.0, ((0, 128),), jnp.float32)
    signs = draw_signs(jax.random.fold_in(streams_of[5], 71), 0)
    samples = draw_samples(jax.random.fold_in(streams_of[5], 71), 0)
    counts = draw_counts(jax.random.fold_in(streams_of[5], 71), 0)
    return dict(panel=panel, logits=logits, signs=signs, samples=samples, counts=counts)


def reference(panel, logits, signs, samples, counts):
    probability = jax.nn.sigmoid(logits)
    root_weight = jnp.sqrt(probability * (1.0 - probability))
    frequency = (jnp.arange(SHARDS, dtype=jnp.int32)[:, None] + SHARDS * samples.astype(jnp.int32)).reshape(-1)
    norm_scale = 1.0 / math.sqrt(ROWS)
    sign_values = signs.astype(jnp.float32)

    def one_column(column):
        signed = column * root_weight * sign_values
        spectrum = jnp.fft.fft(signed)
        chosen = jnp.take(spectrum, frequency)
        return (jnp.real(chosen) - jnp.imag(chosen)) * norm_scale
    picked_rows = lax.map(one_column, panel)
    live_slot = (jnp.arange(SMAX)[None, :] < counts[:, None]).reshape(-1)
    sketch = jnp.where(live_slot[None, :], picked_rows, 0.0)
    gram = jnp.dot(sketch, sketch.T, precision=lax.Precision.HIGHEST)
    sample_total = jnp.sum(counts).astype(jnp.float32)
    lower_factor = jnp.linalg.cholesky(gram / sample_total)
    weighted = panel * root_weight[None, :]
    return lax.linalg.triangular_solve(lower_factor, weighted, left_side=True, lower=True)
```

```python
import functools
import math

import jax
import jax.numpy as jnp
from jax import lax
from jax.experimental import pallas as pl
from jax.experimental.pallas import tpu as pltpu
from jax.sharding import PartitionSpec as P

AXES = ("row", "blk")
LANES = 128
highest = lax.Precision.HIGHEST
f32 = jnp.float32
bf16 = jnp.bfloat16


def split_two(value):
    high = value.astype(bf16)
    low = (value - high.astype(f32)).astype(bf16)
    return high, low


def rounded_parts(value):
    high = lax.reduce_precision(value, 8, 7)
    return high.astype(bf16), (value - high).astype(bf16)


def cos_turns(numerator, length):
    return jnp.cos((2.0 * math.pi / length) * (numerator % length).astype(f32))


def pack_kernel(panel_ref, scale_ref, out_ref):
    lines = panel_ref.shape[0]
    groups = panel_ref.shape[1] // LANES
    for g in range(groups):
        part = panel_ref[:, g * LANES : (g + 1) * LANES] * scale_ref[:, g * LANES : (g + 1) * LANES]
        out_ref[pl.ds(g, lines, stride=groups), :] = part


def pack(panel, scale):
    columns, rows = panel.shape
    groups = rows // LANES
    step = 32
    return pl.pallas_call(
        pack_kernel,
        grid=(columns // step,),
        in_specs=[
            pl.BlockSpec((step, rows), lambda i: (i, 0)),
            pl.BlockSpec((1, rows), lambda i: (0, 0)),
        ],
        out_specs=pl.BlockSpec((step * groups, LANES), lambda i: (i, 0)),
        out_shape=jax.ShapeDtypeStruct((columns * groups, LANES), f32),
        name="pack_columns",
    )(panel, scale)


def phase_kernel(c1_ref, s1_ref, c2_ref, s2_ref, hi_ref, lo_ref):
    for q in range(hi_ref.shape[0]):
        c2 = c2_ref[q]
        s2 = s2_ref[q]
        for a in range(16):
            c1 = c1_ref[q, a : a + 1, :]
            s1 = s1_ref[q, a : a + 1, :]
            re = c1 * c2 - s1 * s2
            im = c1 * s2 + s1 * c2
            hi, lo = split_two(re)
            hi_ref[q, a * 8 : a * 8 + 8, :] = hi
            lo_ref[q, a * 8 : a * 8 + 8, :] = lo
            hi, lo = split_two(im)
            hi_ref[q, 128 + a * 8 : 128 + a * 8 + 8, :] = hi
            lo_ref[q, 128 + a * 8 : 128 + a * 8 + 8, :] = lo


def phase_tables(frequency, total_rows):
    count = frequency.shape[0]
    coarse = frequency[:, None, :] * (8 * jnp.arange(16, dtype=jnp.int32))[None, :, None]
    fine = frequency[:, None, :] * jnp.arange(8, dtype=jnp.int32)[None, :, None]
    coarse = (2.0 * math.pi / total_rows) * (coarse % total_rows).astype(f32)
    fine = (2.0 * math.pi / total_rows) * (fine % total_rows).astype(f32) - 0.25 * math.pi
    root2 = math.sqrt(2.0)
    c1, s1 = jnp.cos(coarse), jnp.sin(coarse)
    c2, s2 = root2 * jnp.cos(fine), root2 * jnp.sin(fine)
    step = 8
    return pl.pallas_call(
        phase_kernel,
        grid=(count // step,),
        in_specs=[
            pl.BlockSpec((step, 16, LANES), lambda i: (i, 0, 0)),
            pl.BlockSpec((step, 16, LANES), lambda i: (i, 0, 0)),
            pl.BlockSpec((step, 8, LANES), lambda i: (i, 0, 0)),
            pl.BlockSpec((step, 8, LANES), lambda i: (i, 0, 0)),
        ],
        out_specs=[pl.BlockSpec((step, 256, LANES), lambda i: (i, 0, 0))] * 2,
        out_shape=[jax.ShapeDtypeStruct((count, 256, LANES), bf16)] * 2,
        name="sample_phases",
    )(c1, s1, c2, s2)


def outer_table(zero):
    o = jnp.arange(128, dtype=jnp.int32)[:, None] + zero
    d = jnp.arange(128, dtype=jnp.int32)[None, :]
    p = o // 2
    odd = o % 2
    wave = jnp.where(o == 1, 64, p)
    quarter = jnp.where((odd == 1) & (p > 0), 32, 0)
    return cos_turns(d * wave - quarter + 128, 128)


def middle_table(zero):
    shape = (64, 2, 2, 32, 2, 32)
    p, cls, part, s1, c, ib = (lax.broadcasted_iota(jnp.int32, shape, k) for k in range(6))
    p = p + zero
    e = jnp.where(cls == 0, p, jnp.where(p == 0, 64, 128 - p))
    angle = ib * (e + 128 * s1)
    quarters = jnp.where(cls == 0, part + c, jnp.where(p == 0, part, jnp.where(c == 0, part, 3 * (1 - part))))
    value = cos_turns(angle + 1024 * quarters, 4096)
    value = jnp.where((p == 0) & (c != cls), 0.0, value)
    return value.reshape(64, 128, 64)


def transform_kernel(outer_ref, data_ref, middle_ref, hi_ref, lo_ref, s1_ref, out_ref, y_ref):
    step = pl.program_id(0)
    pairs = middle_ref.shape[0]

    @pl.when(step == 0)
    def _():
        outer = outer_ref[...]

        def body(i, carry):
            r = i * 2
            left = data_ref[pl.ds(r, 128, stride=64), :]
            right = data_ref[pl.ds(r + 1, 128, stride=64), :]
            both = jnp.concatenate([left, right], axis=1)
            hi, lo = split_two(both)
            res = jnp.dot(outer, jnp.concatenate([hi, lo, hi], axis=0), preferred_element_type=f32)
            y_ref[pl.ds(r, 128, stride=64), :] = res[:, :128]
            y_ref[pl.ds(r + 1, 128, stride=64), :] = res[:, 128:]
            return carry

        lax.fori_loop(0, 32, body, 0)

    for q in range(pairs):
        pair = step * pairs + q
        y = y_ref[pl.ds(pl.multiple_of(pair * 128, 128), 128), :]
        stack = jnp.concatenate(
            [
                jnp.concatenate([y[0:32], y[32:64]], axis=1),
                jnp.concatenate([y[64:96], y[96:128]], axis=1),
            ],
            axis=0,
        )
        hi, lo = split_two(stack)
        z = jnp.dot(middle_ref[q], jnp.concatenate([hi, lo, hi], axis=0), preferred_element_type=f32)
        for cls in range(2):
            zr = z[cls * 64 : cls * 64 + 32]
            zi = z[cls * 64 + 32 : cls * 64 + 64]
            left = jnp.concatenate(
                [
                    jnp.concatenate([zr[:, :128], zi[:, :128]], axis=1),
                    jnp.concatenate([zr[:, 128:], zi[:, 128:]], axis=1),
                ],
                axis=0,
            )
            hi, lo = split_two(left)
            t_hi = hi_ref[2 * q + cls]
            both = jnp.dot(jnp.concatenate([hi, lo], axis=0), t_hi, preferred_element_type=f32)
            res = both[:64] + both[64:] + jnp.dot(hi, lo_ref[2 * q + cls], preferred_element_type=f32)
            row = 2 * q + cls
            wanted = s1_ref[row : row + 1, :]
            mask = lax.broadcasted_iota(jnp.int32, (32, LANES), 0) == wanted
            first = jnp.sum(jnp.where(mask, res[:32], 0.0), axis=0, keepdims=True)
            second = jnp.sum(jnp.where(mask, res[32:], 0.0), axis=0, keepdims=True)
            if cls == 0:
                e = pair
            else:
                e = jnp.where(pair == 0, 64, 128 - pair)
            out_ref[e] = jnp.concatenate([first, second], axis=0)


def transform(data, outer, middle, t_hi, t_lo, s1):
    pairs = 4
    return pl.pallas_call(
        transform_kernel,
        grid=(64 // pairs,),
        in_specs=[
            pl.BlockSpec((128, 384), lambda i: (0, 0)),
            pl.BlockSpec((8192, LANES), lambda i: (0, 0)),
            pl.BlockSpec((pairs, 128, 192), lambda i: (i, 0, 0)),
            pl.BlockSpec((2 * pairs, 256, LANES), lambda i: (i, 0, 0)),
            pl.BlockSpec((2 * pairs, 256, LANES), lambda i: (i, 0, 0)),
            pl.BlockSpec((2 * pairs, LANES), lambda i: (i, 0)),
        ],
        out_specs=pl.BlockSpec((128, 2, LANES), lambda i: (0, 0, 0)),
        out_shape=jax.ShapeDtypeStruct((128, 2, LANES), f32),
        scratch_shapes=[pltpu.VMEM((8192, LANES), f32)],
        compiler_params=pltpu.CompilerParams(vmem_limit_bytes=48 * 1024 * 1024),
        name="sampled_transform",
    )(outer, data, middle, t_hi, t_lo, s1)


def on_device(panel, logits, signs, samples, counts):
    columns, rows_dev = panel.shape
    shards = 128
    total_rows = rows_dev * shards
    slots = samples.shape[1]
    everyone = lax.all_to_all(
        jnp.broadcast_to(jnp.pad(samples, ((0, 0), (0, LANES - slots)))[None], (shards, 1, LANES)),
        AXES,
        split_axis=0,
        concat_axis=0,
        tiled=True,
    ).reshape(shards, LANES)
    probability = jax.nn.sigmoid(logits)
    root_weight = jnp.sqrt(probability * (1.0 - probability))
    packed = pack(panel, (root_weight * signs.astype(f32))[None, :])
    packed, everyone = lax.optimization_barrier((packed, everyone))
    arrived = lax.all_to_all(
        packed.reshape(shards, 64, LANES), AXES, split_axis=0, concat_axis=0, tiled=True
    ).reshape(shards * 64, LANES)

    zero = jnp.minimum(counts[0], 0)
    o_hi, o_lo = rounded_parts(outer_table(zero))
    outer = jnp.concatenate([o_hi, o_hi, o_lo], axis=1)
    m_hi, m_lo = rounded_parts(middle_table(zero))
    middle = jnp.concatenate([m_hi, m_hi, m_lo], axis=2)

    first = everyone[:64]
    second = jnp.concatenate([everyone[64:65], everyone[127:64:-1]], axis=0)
    ordered = jnp.stack([first, second], axis=1).reshape(shards, LANES)
    pair = jnp.arange(64, dtype=jnp.int32)
    residue = jnp.stack([pair, jnp.where(pair == 0, 64, 128 - pair)], axis=1).reshape(shards, 1)
    t_hi, t_lo = phase_tables(residue + shards * ordered, total_rows)

    picked = transform(arrived, outer, middle, t_hi, t_lo, ordered % 32)
    mine = lax.all_to_all(picked, AXES, split_axis=0, concat_axis=0, tiled=True).reshape(columns, LANES)
    live = jnp.arange(LANES, dtype=jnp.int32)[None, :] < counts[0]
    sketch = jnp.where(live, mine * (1.0 / math.sqrt(total_rows)), 0.0)
    gram_part = jnp.dot(sketch, sketch.T, precision=highest)
    corner = (jnp.arange(columns)[:, None] == 0) & (jnp.arange(columns)[None, :] == columns - 1)
    gram_part = jnp.where(corner, counts[0].astype(f32), gram_part)
    lines = columns // shards
    strips = lax.all_to_all(
        gram_part.reshape(shards, lines, columns), AXES, split_axis=0, concat_axis=0, tiled=True
    ).sum(0)
    gram = lax.all_to_all(
        jnp.broadcast_to(strips[None], (shards, lines, columns)), AXES, split_axis=0, concat_axis=0, tiled=True
    ).reshape(columns, columns)
    total = gram[0, columns - 1]
    weighted = panel * root_weight[None, :]
    factor = lax.linalg.cholesky(jnp.tril(gram) / total, symmetrize_input=False)
    return lax.linalg.triangular_solve(factor, weighted, left_side=True, lower=True)


def solution(mesh):
    placed = (
        P(None, AXES),
        P(AXES),
        P(AXES),
        P(AXES, None),
        P(AXES),
    )
    return jax.shard_map(on_device, mesh=mesh, in_specs=placed, out_specs=P(None, AXES), check_vma=False)
```

```python
import functools
import math

import jax
import jax.numpy as jnp
from jax import lax
from jax.experimental import pallas as pl
from jax.experimental.pallas import tpu as pltpu
from jax.sharding import PartitionSpec as P

AXES = ("row", "blk")
LANES = 128
highest = lax.Precision.HIGHEST
f32 = jnp.float32
bf16 = jnp.bfloat16


def split_two(value):
    high = value.astype(bf16)
    low = (value - high.astype(f32)).astype(bf16)
    return high, low


def rounded_parts(value):
    high = lax.reduce_precision(value, 8, 7)
    return high.astype(bf16), (value - high).astype(bf16)


def cos_turns(numerator, length):
    return jnp.cos((2.0 * math.pi / length) * (numerator % length).astype(f32))


def swap_eight(tiles):
    tiles = list(tiles)
    line = lax.broadcasted_iota(jnp.int32, tiles[0].shape, 0)
    for d in (4, 2, 1):
        low = (line & d) == 0
        for i in range(8):
            if i & d == 0:
                first, second = tiles[i], tiles[i + d]
                tiles[i] = jnp.where(low, first, pltpu.roll(second, d, 0))
                tiles[i + d] = jnp.where(low, pltpu.roll(first, 8 - d, 0), second)
    return tiles


def pack_kernel(panel_ref, scale_ref, samples_ref, out_ref):
    lines = panel_ref.shape[0]
    groups = panel_ref.shape[1] // LANES
    for top in range(0, lines, 8):
        for g in range(0, groups, 8):
            spans = [slice((g + i) * LANES, (g + i + 1) * LANES) for i in range(8)]
            tiles = swap_eight([panel_ref[top : top + 8, span] * scale_ref[:, span] for span in spans])
            for i in range(8):
                line = top + i
                row = (line % 2) * groups + g
                out_ref[line // 2, row : row + 8, :] = tiles[i]
    riders = jnp.broadcast_to(samples_ref[...].astype(f32), (8, LANES))
    for q in range(lines // 2):
        out_ref[q, 2 * groups : 2 * groups + 8, :] = riders


def pack(panel, scale, samples):
    columns, rows = panel.shape
    groups = rows // LANES
    step = 32
    return pl.pallas_call(
        pack_kernel,
        grid=(columns // step,),
        in_specs=[
            pl.BlockSpec((step, rows), lambda i: (i, 0)),
            pl.BlockSpec((1, rows), lambda i: (0, 0)),
            pl.BlockSpec((1, LANES), lambda i: (0, 0)),
        ],
        out_specs=pl.BlockSpec((step // 2, 2 * groups + 8, LANES), lambda i: (i, 0, 0)),
        out_shape=jax.ShapeDtypeStruct((columns // 2, 2 * groups + 8, LANES), f32),
        name="pack_columns",
    )(panel, scale, samples)


def unit_circle(step, log_length):
    quarter = log_length - 2
    turn = (step + (1 << (quarter - 1))) >> quarter
    x = (step - (turn << quarter)).astype(f32) * (2.0 * math.pi / (1 << log_length))
    x2 = x * x
    sine = x + x * x2 * (-1 / 6 + x2 * (1 / 120 + x2 * (-1 / 5040 + x2 * (1 / 362880))))
    cosine = 1.0 + x2 * (-0.5 + x2 * (1 / 24 + x2 * (-1 / 720 + x2 * (1 / 40320))))
    odd = (turn & 1) == 1
    a, b = jnp.where(odd, sine, cosine), jnp.where(odd, cosine, sine)
    return jnp.where(((turn + 1) & 2) != 0, -a, a), jnp.where((turn & 2) != 0, -b, b)


def sample_phases(frequency, log_length):
    line = lax.broadcasted_iota(jnp.int32, (8, LANES), 0)
    last = (1 << log_length) - 1
    eighth = 1 << (log_length - 3)
    c2, s2 = unit_circle((frequency * line - eighth) & last, log_length)
    c2, s2 = c2 * math.sqrt(2.0), s2 * math.sqrt(2.0)
    res, ims = [], []
    for half in range(2):
        c8, s8 = unit_circle((frequency * (8 * line + 64 * half)) & last, log_length)
        for a in range(8):
            c1, s1 = c8[a : a + 1], s8[a : a + 1]
            res.append(c1 * c2 - s1 * s2)
            ims.append(c1 * s2 + s1 * c2)
    return jnp.concatenate(res + ims, axis=0)


def middle_table(zero):
    shape = (64, 2, 2, 32, 2, 32)
    p, cls, part, s1, c, ib = (lax.broadcasted_iota(jnp.int32, shape, k) for k in range(6))
    p = p + zero
    e = jnp.where(cls == 0, p, jnp.where(p == 0, 64, 128 - p))
    angle = ib * (e + 128 * s1)
    quarters = jnp.where(cls == 0, part + c, jnp.where(p == 0, part, jnp.where(c == 0, part, 3 * (1 - part))))
    value = cos_turns(angle + 1024 * quarters, 4096)
    value = jnp.where((p == 0) & (c != cls), 0.0, value)
    return value.reshape(64, 128, 64)


def times(value, turn):
    re, im = value
    turn = turn % 1.0
    if turn == 0.0:
        return re, im
    c, s = math.cos(2.0 * math.pi * turn), math.sin(2.0 * math.pi * turn)
    if turn == 0.25:
        return (None if im is None else -im), re
    if turn == 0.5:
        return -re, (None if im is None else -im)
    if im is None:
        return re * c, re * s
    if turn in (0.125, 0.375, 0.625, 0.875):
        root = math.sqrt(0.5)
        plus, minus = (re + im) * root, (re - im) * root
        if turn == 0.125:
            return minus, plus
        if turn == 0.375:
            return -plus, minus
        if turn == 0.625:
            return -minus, -plus
        return plus, -minus
    return re * c - im * s, re * s + im * c


def add(a, b):
    return tuple(y if x is None else (x if y is None else x + y) for x, y in zip(a, b))


def sub(a, b):
    return tuple((None if y is None else -y) if x is None else (x if y is None else x - y) for x, y in zip(a, b))


def small_dft(values):
    length = len(values)
    if length == 1:
        return values
    even, odd = small_dft(values[0::2]), small_dft(values[1::2])
    turned = [times(odd[k], k / length) for k in range(length // 2)]
    return [add(even[k], turned[k]) for k in range(length // 2)] + [sub(even[k], turned[k]) for k in range(length // 2)]


def block_dft(data_ref, y_ref, top):
    inner = [small_dft([(data_ref[16 * n + m], None) for n in range(8)]) for m in range(16)]
    for r in range(5):
        outs = small_dft([times(inner[m][r], m * r / 128) for m in range(16)])
        for f in range(16):
            e = r + 8 * f
            re, im = outs[f]
            if e in (0, 64):
                y_ref[e // 64, pl.ds(top, 8), :] = re
            elif e < 64:
                y_ref[2 * e, pl.ds(top, 8), :] = re
                y_ref[2 * e + 1, pl.ds(top, 8), :] = im
            elif r in (1, 2, 3):
                y_ref[2 * (128 - e), pl.ds(top, 8), :] = re
                y_ref[2 * (128 - e) + 1, pl.ds(top, 8), :] = -im


DATA_STEPS = 8


def transform_kernel(data_ref, rider_ref, middle_ref, out_ref, y_ref, *, log_length):
    step = pl.program_id(0)
    pairs = middle_ref.shape[0]

    @pl.when(step < DATA_STEPS)
    def _():
        block_dft(data_ref, y_ref, pl.multiple_of(step * 8, 8))

    @pl.when(step >= DATA_STEPS)
    def _():
        for q in range(pairs):
            pair = (step - DATA_STEPS) * pairs + q
            cosines = y_ref[2 * pair]
            sines = y_ref[2 * pair + 1]
            stack = jnp.concatenate(
                [
                    jnp.concatenate([cosines[:32], cosines[32:]], axis=1),
                    jnp.concatenate([sines[:32], sines[32:]], axis=1),
                ],
                axis=0,
            )
            hi, lo = split_two(stack)
            mid = middle_ref[q]
            z = jnp.dot(
                jnp.concatenate([mid, mid[:, :64]], axis=1),
                jnp.concatenate([hi, hi, lo], axis=0),
                preferred_element_type=f32,
            )
            for cls in range(2):
                zr = z[cls * 64 : cls * 64 + 32]
                zi = z[cls * 64 + 32 : cls * 64 + 64]
                left = jnp.concatenate(
                    [
                        jnp.concatenate([zr[:, :128], zi[:, :128]], axis=1),
                        jnp.concatenate([zr[:, 128:], zi[:, 128:]], axis=1),
                    ],
                    axis=0,
                )
                hi, lo = split_two(left)
                if cls == 0:
                    e = pair
                else:
                    e = jnp.where(pair == 0, 64, 128 - pair)
                offset = rider_ref[e].astype(jnp.int32)
                t_hi, t_lo = split_two(sample_phases(offset * 128 + e, log_length))
                both = jnp.dot(
                    jnp.concatenate([hi, lo], axis=0),
                    jnp.concatenate([t_hi, t_lo], axis=1),
                    preferred_element_type=f32,
                )
                res = both[:64, :LANES] + both[64:, :LANES] + both[:64, LANES:]
                wanted = jnp.concatenate([offset & 31] * 4, axis=0)
                mask = lax.broadcasted_iota(jnp.int32, (32, LANES), 0) == wanted
                first = jnp.sum(jnp.where(mask, res[:32], 0.0), axis=0, keepdims=True)
                second = jnp.sum(jnp.where(mask, res[32:], 0.0), axis=0, keepdims=True)
                out_ref[e] = jnp.concatenate([first, second], axis=0)


def transform(data, middle, total_rows):
    pairs = 8
    return pl.pallas_call(
        functools.partial(transform_kernel, log_length=total_rows.bit_length() - 1),
        grid=(DATA_STEPS + 64 // pairs,),
        in_specs=[
            pl.BlockSpec((128, 8, LANES), lambda i: (0, jnp.minimum(i, DATA_STEPS - 1), 0)),
            pl.BlockSpec((128, 8, LANES), lambda i: (0, DATA_STEPS, 0)),
            pl.BlockSpec((pairs, 128, 128), lambda i: (jnp.maximum(i - DATA_STEPS, 0), 0, 0)),
        ],
        out_specs=pl.BlockSpec((128, 2, LANES), lambda i: (0, 0, 0)),
        out_shape=jax.ShapeDtypeStruct((128, 2, LANES), f32),
        scratch_shapes=[pltpu.VMEM((128, 64, LANES), f32)],
        compiler_params=pltpu.CompilerParams(vmem_limit_bytes=48 * 1024 * 1024),
        name="sampled_transform",
    )(data, data, middle)


def factor_inverse(a_ref, b_ref):
    size = a_ref.shape[0]
    block = 32
    line = lax.broadcasted_iota(jnp.int32, (8, LANES), 0)
    spread = lambda row: jnp.broadcast_to(row, (8, LANES))
    for lo in range(0, size, block):
        home = lo // LANES
        off = lo % LANES
        spots = [(a_ref, g) for g in range(home, size // LANES)] + [(b_ref, g) for g in range(home + 1)]
        rows = [[ref[lo + 8 * v : lo + 8 * v + 8, g * LANES : (g + 1) * LANES] for ref, g in spots] for v in range(4)]
        pivots = []
        for t in range(4):
            col = [
                {v: jnp.broadcast_to(rows[v][0][:, off + 8 * t + j : off + 8 * t + j + 1], (8, LANES)) for v in range(t, 4)}
                for j in range(8)
            ]
            diag = jnp.ones((8, LANES), f32)
            for j in range(8):
                pivot = spread(col[j][t][j : j + 1])
                inverse = 1.0 / pivot
                diag = jnp.where(line == j, pivot, diag)
                mult = {v: col[j][v] * inverse for v in range(t, 4)}
                mult[t] = jnp.where(line > j, mult[t], 0.0)
                for n in range(j + 1, 8):
                    across = spread(col[j][t][n : n + 1])
                    for v in range(t, 4):
                        col[n][v] = col[n][v] - mult[v] * across
                for g in range(len(spots)):
                    across = spread(rows[t][g][j : j + 1])
                    for v in range(t, 4):
                        rows[v][g] = rows[v][g] - mult[v] * across
            pivots.append(diag)
        for v in range(4):
            scale = lax.rsqrt(pivots[v])
            scale = scale * (1.5 - 0.5 * (pivots[v] * scale) * scale)
            rows[v] = [part * scale for part in rows[v]]
        n_a = size // LANES - home
        for v in range(4):
            for g in range(home + 1):
                b_ref[lo + 8 * v : lo + 8 * v + 8, g * LANES : (g + 1) * LANES] = rows[v][n_a + g]
        if lo + block == size:
            break
        whole = jnp.concatenate([jnp.concatenate(parts, axis=1) for parts in rows], axis=0)
        turned = whole[:, : n_a * LANES].T
        start = lo + block
        cuts = [start, start + block] + ([size] if start + block < size else [])
        for top, end in zip(cuts[:-1], cuts[1:]):
            first = home * LANES
            change = jnp.dot(turned[top - first : end - first], whole, precision=highest, preferred_element_type=f32)
            a_ref[top:end, first:] = a_ref[top:end, first:] - change[:, : n_a * LANES]
            b_ref[top:end, : (home + 1) * LANES] = b_ref[top:end, : (home + 1) * LANES] - change[:, n_a * LANES :]


def finish_kernel(gram_ref, root_ref, panel_ref, out_ref, a_ref, b_ref, w_ref, held_ref, sem):
    size = gram_ref.shape[0]
    width = out_ref.shape[1]

    @pl.when(pl.program_id(0) == 0)
    def _():
        fetch = pltpu.make_async_copy(panel_ref, held_ref, sem)
        fetch.start()
        a_ref[...] = gram_ref[...]
        b_ref[...] = (
            lax.broadcasted_iota(jnp.int32, (size, size), 0) == lax.broadcasted_iota(jnp.int32, (size, size), 1)
        ).astype(f32)
        factor_inverse(a_ref, b_ref)
        total = gram_ref[size - 1 : size, 0:1]
        inverse = b_ref[...] * jnp.sqrt(total)
        high, low = split_two(inverse)
        w_ref[:, :size] = high
        w_ref[:, size : 2 * size] = high
        w_ref[:, 2 * size :] = low
        fetch.wait()

    span = pl.ds(pl.multiple_of(pl.program_id(0) * width, width), width)
    high, low = split_two(held_ref[:, span] * root_ref[...])
    out_ref[...] = jnp.dot(w_ref[...], jnp.concatenate([high, low, high], axis=0), preferred_element_type=f32)


def finish(gram, root_weight, panel):
    columns, rows = panel.shape
    width = 512
    return pl.pallas_call(
        finish_kernel,
        grid=(rows // width,),
        in_specs=[
            pl.BlockSpec((columns, columns), lambda i: (0, 0)),
            pl.BlockSpec((1, width), lambda i: (0, i)),
            pl.BlockSpec(memory_space=pl.ANY),
        ],
        out_specs=pl.BlockSpec((columns, width), lambda i: (0, i)),
        out_shape=jax.ShapeDtypeStruct((columns, rows), f32),
        scratch_shapes=[
            pltpu.VMEM((columns, columns), f32),
            pltpu.VMEM((columns, columns), f32),
            pltpu.VMEM((columns, 3 * columns), bf16),
            pltpu.VMEM((columns, rows), f32),
            pltpu.SemaphoreType.DMA,
        ],
        compiler_params=pltpu.CompilerParams(vmem_limit_bytes=48 * 1024 * 1024),
        name="factor_and_apply",
    )(gram, root_weight, pltpu.with_memory_space_constraint(panel, pltpu.HBM))


def on_device(panel, logits, signs, samples, counts):
    columns, rows_dev = panel.shape
    shards = 128
    total_rows = rows_dev * shards
    slots = samples.shape[1]
    probability = jax.nn.sigmoid(logits)
    root_weight = jnp.sqrt(probability * (1.0 - probability))
    packed = pack(
        panel,
        (root_weight * signs.astype(f32))[None, :],
        jnp.pad(samples, ((0, 0), (0, LANES - slots))),
    )
    arrived = lax.all_to_all(packed, AXES, split_axis=0, concat_axis=0, tiled=True)

    zero = jnp.minimum(counts[0], 0)
    m_hi, m_lo = rounded_parts(middle_table(zero))
    middle = jnp.concatenate([m_hi, m_lo], axis=2)

    picked = transform(arrived, middle, total_rows)
    mine = lax.all_to_all(picked, AXES, split_axis=0, concat_axis=0, tiled=True).reshape(columns, LANES)
    live = jnp.arange(LANES, dtype=jnp.int32)[None, :] < counts[0]
    sketch = jnp.where(live, mine * (1.0 / math.sqrt(total_rows)), 0.0)
    gram_part = jnp.dot(sketch, sketch.T, precision=highest)
    corner = (jnp.arange(columns)[:, None] == columns - 1) & (jnp.arange(columns)[None, :] == 0)
    gram_part = jnp.where(corner, counts[0].astype(f32), gram_part)
    lines = columns // shards
    strips = lax.all_to_all(
        gram_part.reshape(shards, lines, columns), AXES, split_axis=0, concat_axis=0, tiled=True
    ).sum(0)
    gram = lax.all_to_all(
        jnp.broadcast_to(strips[None], (shards, lines, columns)), AXES, split_axis=0, concat_axis=0, tiled=True
    ).reshape(columns, columns)
    return finish(gram, root_weight[None, :], panel)


def solution(mesh):
    placed = (
        P(None, AXES),
        P(AXES),
        P(AXES),
        P(AXES, None),
        P(AXES),
    )
    return jax.shard_map(on_device, mesh=mesh, in_specs=placed, out_specs=P(None, AXES), check_vma=False)
```

```python
import functools
import math

import jax
import jax.numpy as jnp
from jax import lax
from jax.experimental import pallas as pl
from jax.experimental.pallas import tpu as pltpu
from jax.sharding import PartitionSpec as P

AXES = ("row", "blk")
LANES = 128
highest = lax.Precision.HIGHEST
f32 = jnp.float32
bf16 = jnp.bfloat16


def split_two(value):
    high = value.astype(bf16)
    low = (value - high.astype(f32)).astype(bf16)
    return high, low


def rounded_parts(value):
    high = lax.reduce_precision(value, 8, 7)
    return high.astype(bf16), (value - high).astype(bf16)


def cos_turns(numerator, length):
    return jnp.cos((2.0 * math.pi / length) * (numerator % length).astype(f32))


def swap_eight(tiles):
    tiles = list(tiles)
    line = lax.broadcasted_iota(jnp.int32, tiles[0].shape, 0)
    for d in (4, 2, 1):
        low = (line & d) == 0
        for i in range(8):
            if i & d == 0:
                first, second = tiles[i], tiles[i + d]
                tiles[i] = jnp.where(low, first, pltpu.roll(second, d, 0))
                tiles[i + d] = jnp.where(low, pltpu.roll(first, 8 - d, 0), second)
    return tiles


def pack_kernel(panel_ref, logits_ref, signs_ref, samples_ref, out_ref, root_ref, scale_ref, rider_ref):
    lines = panel_ref.shape[0]
    groups = panel_ref.shape[1] // LANES
    slots = samples_ref.shape[1]

    @pl.when(pl.program_id(0) == 0)
    def _():
        probability = 1.0 / (1.0 + jnp.exp(-logits_ref[...]))
        root = jnp.sqrt(probability * (1.0 - probability))
        root_ref[...] = root
        scale_ref[...] = root * signs_ref[...].astype(f32)
        rider_ref[...] = jnp.zeros_like(rider_ref)
        rider_ref[:, :slots] = jnp.broadcast_to(samples_ref[...].astype(f32), (8, slots))

    for top in range(0, lines, 8):
        for g in range(0, groups, 8):
            spans = [slice((g + i) * LANES, (g + i + 1) * LANES) for i in range(8)]
            tiles = swap_eight([panel_ref[top : top + 8, span] * scale_ref[:, span] for span in spans])
            for i in range(8):
                line = top + i
                row = (line % 2) * groups + g
                out_ref[line // 2, row : row + 8, :] = tiles[i]
    for q in range(lines // 2):
        out_ref[q, 2 * groups : 2 * groups + 8, :] = rider_ref[...]


def pack(panel, logits, signs, samples):
    columns, rows = panel.shape
    groups = rows // LANES
    step = 128
    whole = pl.BlockSpec((1, rows), lambda i: (0, 0))
    return pl.pallas_call(
        pack_kernel,
        grid=(columns // step,),
        in_specs=[
            pl.BlockSpec((step, rows), lambda i: (i, 0)),
            whole,
            whole,
            pl.BlockSpec(samples.shape, lambda i: (0, 0)),
        ],
        out_specs=[pl.BlockSpec((step // 2, 2 * groups + 8, LANES), lambda i: (i, 0, 0)), whole],
        out_shape=[
            jax.ShapeDtypeStruct((columns // 2, 2 * groups + 8, LANES), f32),
            jax.ShapeDtypeStruct((1, rows), f32),
        ],
        scratch_shapes=[pltpu.VMEM((1, rows), f32), pltpu.VMEM((8, LANES), f32)],
        name="pack_columns",
    )(panel, logits, signs, samples)


def unit_circle(step, log_length):
    quarter = log_length - 2
    turn = (step + (1 << (quarter - 1))) >> quarter
    x = (step - (turn << quarter)).astype(f32) * (2.0 * math.pi / (1 << log_length))
    x2 = x * x
    sine = x + x * x2 * (-1 / 6 + x2 * (1 / 120 + x2 * (-1 / 5040 + x2 * (1 / 362880))))
    cosine = 1.0 + x2 * (-0.5 + x2 * (1 / 24 + x2 * (-1 / 720 + x2 * (1 / 40320))))
    odd = (turn & 1) == 1
    a, b = jnp.where(odd, sine, cosine), jnp.where(odd, cosine, sine)
    return jnp.where(((turn + 1) & 2) != 0, -a, a), jnp.where((turn & 2) != 0, -b, b)


def sample_phases(frequency, log_length):
    line = lax.broadcasted_iota(jnp.int32, (8, LANES), 0)
    last = (1 << log_length) - 1
    eighth = 1 << (log_length - 3)
    c2, s2 = unit_circle((frequency * line - eighth) & last, log_length)
    c2, s2 = c2 * math.sqrt(2.0), s2 * math.sqrt(2.0)
    res, ims = [], []
    for half in range(2):
        c8, s8 = unit_circle((frequency * (8 * line + 64 * half)) & last, log_length)
        for a in range(8):
            c1, s1 = c8[a : a + 1], s8[a : a + 1]
            res.append(c1 * c2 - s1 * s2)
            ims.append(c1 * s2 + s1 * c2)
    return jnp.concatenate(res + ims, axis=0)


def middle_table(zero):
    shape = (64, 2, 2, 32, 2, 32)
    p, cls, part, s1, c, ib = (lax.broadcasted_iota(jnp.int32, shape, k) for k in range(6))
    p = p + zero
    e = jnp.where(cls == 0, p, jnp.where(p == 0, 64, 128 - p))
    angle = ib * (e + 128 * s1)
    quarters = jnp.where(cls == 0, part + c, jnp.where(p == 0, part, jnp.where(c == 0, part, 3 * (1 - part))))
    value = cos_turns(angle + 1024 * quarters, 4096)
    value = jnp.where((p == 0) & (c != cls), 0.0, value)
    return value.reshape(64, 128, 64)


def times(value, turn):
    re, im = value
    turn = turn % 1.0
    if turn == 0.0:
        return re, im
    c, s = math.cos(2.0 * math.pi * turn), math.sin(2.0 * math.pi * turn)
    if turn == 0.25:
        return (None if im is None else -im), re
    if turn == 0.5:
        return -re, (None if im is None else -im)
    if im is None:
        return re * c, re * s
    if turn in (0.125, 0.375, 0.625, 0.875):
        root = math.sqrt(0.5)
        plus, minus = (re + im) * root, (re - im) * root
        if turn == 0.125:
            return minus, plus
        if turn == 0.375:
            return -plus, minus
        if turn == 0.625:
            return -minus, -plus
        return plus, -minus
    return re * c - im * s, re * s + im * c


def add(a, b):
    return tuple(y if x is None else (x if y is None else x + y) for x, y in zip(a, b))


def sub(a, b):
    return tuple((None if y is None else -y) if x is None else (x if y is None else x - y) for x, y in zip(a, b))


def small_dft(values):
    length = len(values)
    if length == 1:
        return values
    even, odd = small_dft(values[0::2]), small_dft(values[1::2])
    turned = [times(odd[k], k / length) for k in range(length // 2)]
    return [add(even[k], turned[k]) for k in range(length // 2)] + [sub(even[k], turned[k]) for k in range(length // 2)]


def block_dft(data_ref, part, y_ref, top):
    inner = [small_dft([(data_ref[16 * n + m, part : part + 8], None) for n in range(8)]) for m in range(16)]
    for r in range(5):
        outs = small_dft([times(inner[m][r], m * r / 128) for m in range(16)])
        for f in range(16):
            e = r + 8 * f
            re, im = outs[f]
            if e in (0, 64):
                y_ref[e // 64, pl.ds(top, 8), :] = re
            elif e < 64:
                y_ref[2 * e, pl.ds(top, 8), :] = re
                y_ref[2 * e + 1, pl.ds(top, 8), :] = im
            elif r in (1, 2, 3):
                y_ref[2 * (128 - e), pl.ds(top, 8), :] = re
                y_ref[2 * (128 - e) + 1, pl.ds(top, 8), :] = -im


DATA_STEPS = 4


def transform_kernel(data_ref, rider_ref, middle_ref, out_ref, y_ref, *, log_length):
    step = pl.program_id(0)
    pairs = middle_ref.shape[0]

    @pl.when(step < DATA_STEPS)
    def _():
        for part in range(0, data_ref.shape[1], 8):
            block_dft(data_ref, part, y_ref, pl.multiple_of(step * data_ref.shape[1] + part, 8))

    @pl.when(step >= DATA_STEPS)
    def _():
        products = []
        for q in range(pairs):
            pair = (step - DATA_STEPS) * pairs + q
            cosines = y_ref[2 * pair]
            sines = y_ref[2 * pair + 1]
            stack = jnp.concatenate(
                [
                    jnp.concatenate([cosines[:32], cosines[32:]], axis=1),
                    jnp.concatenate([sines[:32], sines[32:]], axis=1),
                ],
                axis=0,
            )
            hi, lo = split_two(stack)
            mid = middle_ref[q]
            z = jnp.dot(
                jnp.concatenate([mid, mid[:, :64]], axis=1),
                jnp.concatenate([hi, hi, lo], axis=0),
                preferred_element_type=f32,
            )
            products.append(z)
        for q in range(pairs):
            z = products[q]
            pair = (step - DATA_STEPS) * pairs + q
            for cls in range(2):
                zr = z[cls * 64 : cls * 64 + 32]
                zi = z[cls * 64 + 32 : cls * 64 + 64]
                left = jnp.concatenate(
                    [
                        jnp.concatenate([zr[:, :128], zi[:, :128]], axis=1),
                        jnp.concatenate([zr[:, 128:], zi[:, 128:]], axis=1),
                    ],
                    axis=0,
                )
                hi, lo = split_two(left)
                if cls == 0:
                    e = pair
                else:
                    e = jnp.where(pair == 0, 64, 128 - pair)
                offset = rider_ref[e].astype(jnp.int32)
                t_hi, t_lo = split_two(sample_phases(offset * 128 + e, log_length))
                both = jnp.dot(
                    jnp.concatenate([hi, lo], axis=0),
                    jnp.concatenate([t_hi, t_lo], axis=1),
                    preferred_element_type=f32,
                )
                res = both[:64, :LANES] + both[64:, :LANES] + both[:64, LANES:]
                wanted = jnp.concatenate([offset & 31] * 4, axis=0)
                mask = lax.broadcasted_iota(jnp.int32, (32, LANES), 0) == wanted
                first = jnp.sum(jnp.where(mask, res[:32], 0.0), axis=0, keepdims=True)
                second = jnp.sum(jnp.where(mask, res[32:], 0.0), axis=0, keepdims=True)
                out_ref[e] = jnp.concatenate([first, second], axis=0)


def transform(data, middle, total_rows):
    pairs = 8
    rows = data.shape[1] - 8
    return pl.pallas_call(
        functools.partial(transform_kernel, log_length=total_rows.bit_length() - 1),
        grid=(DATA_STEPS + 64 // pairs,),
        in_specs=[
            pl.BlockSpec((128, rows // DATA_STEPS, LANES), lambda i: (0, jnp.minimum(i, DATA_STEPS - 1), 0)),
            pl.BlockSpec((128, 8, LANES), lambda i: (0, rows // 8, 0)),
            pl.BlockSpec((pairs, 128, 128), lambda i: (jnp.maximum(i - DATA_STEPS, 0), 0, 0)),
        ],
        out_specs=pl.BlockSpec((128, 2, LANES), lambda i: (0, 0, 0)),
        out_shape=jax.ShapeDtypeStruct((128, 2, LANES), f32),
        scratch_shapes=[pltpu.VMEM((128, 64, LANES), f32)],
        compiler_params=pltpu.CompilerParams(vmem_limit_bytes=48 * 1024 * 1024),
        name="sampled_transform",
    )(data, data, middle)


def factor_inverse(a_ref, b_ref):
    size = a_ref.shape[0]
    block = 32
    line = lax.broadcasted_iota(jnp.int32, (8, LANES), 0)
    spread = lambda row: jnp.broadcast_to(row, (8, LANES))
    for lo in range(0, size, block):
        home = lo // LANES
        off = lo % LANES
        spots = [(a_ref, g) for g in range(home, size // LANES)] + [(b_ref, g) for g in range(home + 1)]
        rows = [[ref[lo + 8 * v : lo + 8 * v + 8, g * LANES : (g + 1) * LANES] for ref, g in spots] for v in range(4)]
        pivots = []
        for t in range(4):
            col = [
                {v: jnp.broadcast_to(rows[v][0][:, off + 8 * t + j : off + 8 * t + j + 1], (8, LANES)) for v in range(t, 4)}
                for j in range(8)
            ]
            diag = jnp.ones((8, LANES), f32)
            for j in range(8):
                pivot = spread(col[j][t][j : j + 1])
                inverse = 1.0 / pivot
                diag = jnp.where(line == j, pivot, diag)
                mult = {v: col[j][v] * inverse for v in range(t, 4)}
                mult[t] = jnp.where(line > j, mult[t], 0.0)
                for n in range(j + 1, 8):
                    across = spread(col[j][t][n : n + 1])
                    for v in range(t, 4):
                        col[n][v] = col[n][v] - mult[v] * across
                for g in range(len(spots)):
                    across = spread(rows[t][g][j : j + 1])
                    for v in range(t, 4):
                        rows[v][g] = rows[v][g] - mult[v] * across
            pivots.append(diag)
        for v in range(4):
            scale = lax.rsqrt(pivots[v])
            scale = scale * (1.5 - 0.5 * (pivots[v] * scale) * scale)
            rows[v] = [part * scale for part in rows[v]]
        n_a = size // LANES - home
        for v in range(4):
            for g in range(home + 1):
                b_ref[lo + 8 * v : lo + 8 * v + 8, g * LANES : (g + 1) * LANES] = rows[v][n_a + g]
        if lo + block == size:
            break
        whole = jnp.concatenate([jnp.concatenate(parts, axis=1) for parts in rows], axis=0)
        turned = whole[:, : n_a * LANES].T
        start = lo + block
        cuts = [start, start + block] + ([size] if start + block < size else [])
        for top, end in zip(cuts[:-1], cuts[1:]):
            first = home * LANES
            change = jnp.dot(turned[top - first : end - first], whole, precision=highest, preferred_element_type=f32)
            a_ref[top:end, first:] = a_ref[top:end, first:] - change[:, : n_a * LANES]
            b_ref[top:end, : (home + 1) * LANES] = b_ref[top:end, : (home + 1) * LANES] - change[:, n_a * LANES :]


def finish_kernel(gram_ref, root_ref, panel_ref, out_ref, a_ref, b_ref, w_ref, held_ref, sem):
    size = gram_ref.shape[0]
    width = out_ref.shape[1]

    @pl.when(pl.program_id(0) == 0)
    def _():
        fetch = pltpu.make_async_copy(panel_ref, held_ref, sem)
        fetch.start()
        a_ref[...] = gram_ref[...]
        b_ref[...] = (
            lax.broadcasted_iota(jnp.int32, (size, size), 0) == lax.broadcasted_iota(jnp.int32, (size, size), 1)
        ).astype(f32)
        factor_inverse(a_ref, b_ref)
        total = gram_ref[size - 1 : size, 0:1]
        inverse = b_ref[...] * jnp.sqrt(total)
        high, low = split_two(inverse)
        w_ref[:, :size] = high
        w_ref[:, size : 2 * size] = high
        w_ref[:, 2 * size :] = low
        fetch.wait()

    span = pl.ds(pl.multiple_of(pl.program_id(0) * width, width), width)
    high, low = split_two(held_ref[:, span] * root_ref[...])
    out_ref[...] = jnp.dot(w_ref[...], jnp.concatenate([high, low, high], axis=0), preferred_element_type=f32)


def finish(gram, root_weight, panel):
    columns, rows = panel.shape
    width = 2048
    return pl.pallas_call(
        finish_kernel,
        grid=(rows // width,),
        in_specs=[
            pl.BlockSpec((columns, columns), lambda i: (0, 0)),
            pl.BlockSpec((1, width), lambda i: (0, i)),
            pl.BlockSpec(memory_space=pl.ANY),
        ],
        out_specs=pl.BlockSpec((columns, width), lambda i: (0, i)),
        out_shape=jax.ShapeDtypeStruct((columns, rows), f32),
        scratch_shapes=[
            pltpu.VMEM((columns, columns), f32),
            pltpu.VMEM((columns, columns), f32),
            pltpu.VMEM((columns, 3 * columns), bf16),
            pltpu.VMEM((columns, rows), f32),
            pltpu.SemaphoreType.DMA,
        ],
        compiler_params=pltpu.CompilerParams(vmem_limit_bytes=48 * 1024 * 1024),
        name="factor_and_apply",
    )(gram, root_weight, pltpu.with_memory_space_constraint(panel, pltpu.HBM))


def on_device(panel, logits, signs, samples, counts):
    columns, rows_dev = panel.shape
    shards = 128
    total_rows = rows_dev * shards
    packed, root_weight = pack(panel, logits[None, :], signs[None, :], samples)
    arrived = lax.all_to_all(packed, AXES, split_axis=0, concat_axis=0, tiled=True)

    zero = jnp.minimum(counts[0], 0)
    m_hi, m_lo = rounded_parts(middle_table(zero))
    middle = jnp.concatenate([m_hi, m_lo], axis=2)

    picked = transform(arrived, middle, total_rows)
    mine = lax.all_to_all(picked, AXES, split_axis=0, concat_axis=0, tiled=True).reshape(columns, LANES)
    live = jnp.arange(LANES, dtype=jnp.int32)[None, :] < counts[0]
    sketch = jnp.where(live, mine * (1.0 / math.sqrt(total_rows)), 0.0)
    gram_part = jnp.dot(sketch, sketch.T, precision=highest)
    corner = (jnp.arange(columns)[:, None] == columns - 1) & (jnp.arange(columns)[None, :] == 0)
    gram_part = jnp.where(corner, counts[0].astype(f32), gram_part)
    lines = columns // shards
    strips = lax.all_to_all(
        gram_part.reshape(shards, lines, columns), AXES, split_axis=0, concat_axis=0, tiled=True
    ).sum(0)
    gram = lax.all_to_all(
        jnp.broadcast_to(strips[None], (shards, lines, columns)), AXES, split_axis=0, concat_axis=0, tiled=True
    ).reshape(columns, columns)
    return finish(gram, root_weight, panel)


def solution(mesh):
    placed = (
        P(None, AXES),
        P(AXES),
        P(AXES),
        P(AXES, None),
        P(AXES),
    )
    return jax.shard_map(on_device, mesh=mesh, in_specs=placed, out_specs=P(None, AXES), check_vma=False)
```

```python
import functools
import math

import jax
import jax.numpy as jnp
from jax import lax
from jax.experimental import pallas as pl
from jax.experimental.pallas import tpu as pltpu
from jax.sharding import PartitionSpec as P

AXES = ("row", "blk")
LANES = 128
highest = lax.Precision.HIGHEST
f32 = jnp.float32
bf16 = jnp.bfloat16


def split_two(value):
    high = value.astype(bf16)
    low = (value - high.astype(f32)).astype(bf16)
    return high, low


def rounded_parts(value):
    high = lax.reduce_precision(value, 8, 7)
    return high.astype(bf16), (value - high).astype(bf16)


def cos_turns(numerator, length):
    return jnp.cos((2.0 * math.pi / length) * (numerator % length).astype(f32))


def swap_eight(tiles):
    tiles = list(tiles)
    line = lax.broadcasted_iota(jnp.int32, tiles[0].shape, 0)
    for d in (4, 2, 1):
        low = (line & d) == 0
        for i in range(8):
            if i & d == 0:
                first, second = tiles[i], tiles[i + d]
                tiles[i] = jnp.where(low, first, pltpu.roll(second, d, 0))
                tiles[i + d] = jnp.where(low, pltpu.roll(first, 8 - d, 0), second)
    return tiles


def pack_kernel(panel_ref, logits_ref, signs_ref, samples_ref, out_ref, root_ref, scale_ref, rider_ref):
    lines = panel_ref.shape[0]
    groups = panel_ref.shape[1] // LANES
    slots = samples_ref.shape[1]

    @pl.when(pl.program_id(0) == 0)
    def _():
        probability = 1.0 / (1.0 + jnp.exp(-logits_ref[...]))
        root = jnp.sqrt(probability * (1.0 - probability))
        root_ref[...] = root
        scale_ref[...] = root * signs_ref[...].astype(f32)
        rider_ref[...] = jnp.zeros_like(rider_ref)
        rider_ref[:, :slots] = jnp.broadcast_to(samples_ref[...].astype(f32), (8, slots))

    for top in range(0, lines, 8):
        for g in range(0, groups, 8):
            spans = [slice((g + i) * LANES, (g + i + 1) * LANES) for i in range(8)]
            tiles = swap_eight([panel_ref[top : top + 8, span] * scale_ref[:, span] for span in spans])
            for i in range(8):
                line = top + i
                row = (line // 2) * (2 * groups + 1) + (line % 2) * groups + g
                out_ref[row : row + 8, :] = tiles[i]
    for q in range(lines // 2):
        row = (q + 1) * (2 * groups + 1) - 1
        out_ref[row : row + 1, :] = rider_ref[:1]


def pack(panel, logits, signs, samples):
    columns, rows = panel.shape
    groups = rows // LANES
    step = 128
    whole = pl.BlockSpec((1, rows), lambda i: (0, 0))
    return pl.pallas_call(
        pack_kernel,
        grid=(columns // step,),
        in_specs=[
            pl.BlockSpec((step, rows), lambda i: (i, 0)),
            whole,
            whole,
            pl.BlockSpec(samples.shape, lambda i: (0, 0)),
        ],
        out_specs=[pl.BlockSpec((step // 2 * (2 * groups + 1), LANES), lambda i: (i, 0)), whole],
        out_shape=[
            jax.ShapeDtypeStruct((columns // 2 * (2 * groups + 1), LANES), f32),
            jax.ShapeDtypeStruct((1, rows), f32),
        ],
        scratch_shapes=[pltpu.VMEM((1, rows), f32), pltpu.VMEM((8, LANES), f32)],
        name="pack_columns",
    )(panel, logits, signs, samples)


def unit_circle(step, log_length):
    quarter = log_length - 2
    turn = (step + (1 << (quarter - 1))) >> quarter
    x = (step - (turn << quarter)).astype(f32) * (2.0 * math.pi / (1 << log_length))
    x2 = x * x
    sine = x + x * x2 * (-1 / 6 + x2 * (1 / 120 + x2 * (-1 / 5040 + x2 * (1 / 362880))))
    cosine = 1.0 + x2 * (-0.5 + x2 * (1 / 24 + x2 * (-1 / 720 + x2 * (1 / 40320))))
    odd = (turn & 1) == 1
    a, b = jnp.where(odd, sine, cosine), jnp.where(odd, cosine, sine)
    return jnp.where(((turn + 1) & 2) != 0, -a, a), jnp.where((turn & 2) != 0, -b, b)


def sample_phases(frequency, log_length):
    line = lax.broadcasted_iota(jnp.int32, (8, LANES), 0)
    last = (1 << log_length) - 1
    eighth = 1 << (log_length - 3)
    c2, s2 = unit_circle((frequency * line - eighth) & last, log_length)
    c2, s2 = c2 * math.sqrt(2.0), s2 * math.sqrt(2.0)
    res, ims = [], []
    for half in range(2):
        c8, s8 = unit_circle((frequency * (8 * line + 64 * half)) & last, log_length)
        for a in range(8):
            c1, s1 = c8[a : a + 1], s8[a : a + 1]
            res.append(c1 * c2 - s1 * s2)
            ims.append(c1 * s2 + s1 * c2)
    return jnp.concatenate(res + ims, axis=0)


def middle_table(zero):
    shape = (64, 2, 2, 32, 2, 32)
    p, cls, part, s1, c, ib = (lax.broadcasted_iota(jnp.int32, shape, k) for k in range(6))
    p = p + zero
    e = jnp.where(cls == 0, p, jnp.where(p == 0, 64, 128 - p))
    angle = ib * (e + 128 * s1)
    quarters = jnp.where(cls == 0, part + c, jnp.where(p == 0, part, jnp.where(c == 0, part, 3 * (1 - part))))
    value = cos_turns(angle + 1024 * quarters, 4096)
    value = jnp.where((p == 0) & (c != cls), 0.0, value)
    return value.reshape(64, 128, 64)


def times(value, turn):
    re, im = value
    turn = turn % 1.0
    if turn == 0.0:
        return re, im
    c, s = math.cos(2.0 * math.pi * turn), math.sin(2.0 * math.pi * turn)
    if turn == 0.25:
        return (None if im is None else -im), re
    if turn == 0.5:
        return -re, (None if im is None else -im)
    if im is None:
        return re * c, re * s
    if turn in (0.125, 0.375, 0.625, 0.875):
        root = math.sqrt(0.5)
        plus, minus = (re + im) * root, (re - im) * root
        if turn == 0.125:
            return minus, plus
        if turn == 0.375:
            return -plus, minus
        if turn == 0.625:
            return -minus, -plus
        return plus, -minus
    return re * c - im * s, re * s + im * c


def add(a, b):
    return tuple(y if x is None else (x if y is None else x + y) for x, y in zip(a, b))


def sub(a, b):
    return tuple((None if y is None else -y) if x is None else (x if y is None else x - y) for x, y in zip(a, b))


def small_dft(values):
    length = len(values)
    if length == 1:
        return values
    even, odd = small_dft(values[0::2]), small_dft(values[1::2])
    turned = [times(odd[k], k / length) for k in range(length // 2)]
    return [add(even[k], turned[k]) for k in range(length // 2)] + [sub(even[k], turned[k]) for k in range(length // 2)]


def block_dft(data_ref, part, y_ref, top):
    inner = [small_dft([(data_ref[(16 * n + m) * 65 + part : (16 * n + m) * 65 + part + 8], None) for n in range(8)]) for m in range(16)]
    for r in range(5):
        outs = small_dft([times(inner[m][r], m * r / 128) for m in range(16)])
        for f in range(16):
            e = r + 8 * f
            re, im = outs[f]
            if e in (0, 64):
                y_ref[e // 64, pl.ds(top, 8), :] = re
            elif e < 64:
                y_ref[2 * e, pl.ds(top, 8), :] = re
                y_ref[2 * e + 1, pl.ds(top, 8), :] = im
            elif r in (1, 2, 3):
                y_ref[2 * (128 - e), pl.ds(top, 8), :] = re
                y_ref[2 * (128 - e) + 1, pl.ds(top, 8), :] = -im


DATA_STEPS = 1


def transform_kernel(data_ref, middle_ref, out_ref, y_ref, *, log_length):
    step = pl.program_id(0)
    pairs = middle_ref.shape[0]

    @pl.when(step < DATA_STEPS)
    def _():
        for part in range(0, 64, 8):
            block_dft(data_ref, part, y_ref, part)

    @pl.when(step >= DATA_STEPS)
    def _():
        products = []
        for q in range(pairs):
            pair = (step - DATA_STEPS) * pairs + q
            cosines = y_ref[2 * pair]
            sines = y_ref[2 * pair + 1]
            stack = jnp.concatenate(
                [
                    jnp.concatenate([cosines[:32], cosines[32:]], axis=1),
                    jnp.concatenate([sines[:32], sines[32:]], axis=1),
                ],
                axis=0,
            )
            hi, lo = split_two(stack)
            mid = middle_ref[q]
            z = jnp.dot(
                jnp.concatenate([mid, mid[:, :64]], axis=1),
                jnp.concatenate([hi, hi, lo], axis=0),
                preferred_element_type=f32,
            )
            products.append(z)
        for q in range(pairs):
            z = products[q]
            pair = (step - DATA_STEPS) * pairs + q
            for cls in range(2):
                zr = z[cls * 64 : cls * 64 + 32]
                zi = z[cls * 64 + 32 : cls * 64 + 64]
                left = jnp.concatenate(
                    [
                        jnp.concatenate([zr[:, :128], zi[:, :128]], axis=1),
                        jnp.concatenate([zr[:, 128:], zi[:, 128:]], axis=1),
                    ],
                    axis=0,
                )
                hi, lo = split_two(left)
                if cls == 0:
                    e = pair
                else:
                    e = jnp.where(pair == 0, 64, 128 - pair)
                offset = jnp.broadcast_to(data_ref[pl.ds(e * 65 + 64, 1), :].astype(jnp.int32), (8, LANES))
                t_hi, t_lo = split_two(sample_phases(offset * 128 + e, log_length))
                both = jnp.dot(
                    jnp.concatenate([hi, lo], axis=0),
                    jnp.concatenate([t_hi, t_lo], axis=1),
                    preferred_element_type=f32,
                )
                res = both[:64, :LANES] + both[64:, :LANES] + both[:64, LANES:]
                wanted = jnp.concatenate([offset & 31] * 4, axis=0)
                mask = lax.broadcasted_iota(jnp.int32, (32, LANES), 0) == wanted
                first = jnp.sum(jnp.where(mask, res[:32], 0.0), axis=0, keepdims=True)
                second = jnp.sum(jnp.where(mask, res[32:], 0.0), axis=0, keepdims=True)
                out_ref[e] = jnp.concatenate([first, second], axis=0)


def transform(data, middle, total_rows):
    pairs = 8
    return pl.pallas_call(
        functools.partial(transform_kernel, log_length=total_rows.bit_length() - 1),
        grid=(DATA_STEPS + 64 // pairs,),
        in_specs=[
            pl.BlockSpec(data.shape, lambda i: (0, 0)),
            pl.BlockSpec((pairs, 128, 128), lambda i: (jnp.maximum(i - DATA_STEPS, 0), 0, 0)),
        ],
        out_specs=pl.BlockSpec((128, 2, LANES), lambda i: (0, 0, 0)),
        out_shape=jax.ShapeDtypeStruct((128, 2, LANES), f32),
        scratch_shapes=[pltpu.VMEM((128, 64, LANES), f32)],
        compiler_params=pltpu.CompilerParams(vmem_limit_bytes=48 * 1024 * 1024),
        name="sampled_transform",
    )(data, middle)


def factor_inverse(a_ref, b_ref):
    size = a_ref.shape[0]
    block = 32
    line = lax.broadcasted_iota(jnp.int32, (8, LANES), 0)
    spread = lambda row: jnp.broadcast_to(row, (8, LANES))
    for lo in range(0, size, block):
        home = lo // LANES
        off = lo % LANES
        spots = [(a_ref, g) for g in range(home, size // LANES)] + [(b_ref, g) for g in range(home + 1)]
        rows = [[ref[lo + 8 * v : lo + 8 * v + 8, g * LANES : (g + 1) * LANES] for ref, g in spots] for v in range(4)]
        pivots = []
        for t in range(4):
            col = [
                {v: jnp.broadcast_to(rows[v][0][:, off + 8 * t + j : off + 8 * t + j + 1], (8, LANES)) for v in range(t, 4)}
                for j in range(8)
            ]
            diag = jnp.ones((8, LANES), f32)
            for j in range(8):
                pivot = spread(col[j][t][j : j + 1])
                inverse = 1.0 / pivot
                diag = jnp.where(line == j, pivot, diag)
                mult = {v: col[j][v] * inverse for v in range(t, 4)}
                mult[t] = jnp.where(line > j, mult[t], 0.0)
                for n in range(j + 1, 8):
                    across = spread(col[j][t][n : n + 1])
                    for v in range(t, 4):
                        col[n][v] = col[n][v] - mult[v] * across
                for g in range(len(spots)):
                    across = spread(rows[t][g][j : j + 1])
                    for v in range(t, 4):
                        rows[v][g] = rows[v][g] - mult[v] * across
            pivots.append(diag)
        for v in range(4):
            scale = lax.rsqrt(pivots[v])
            scale = scale * (1.5 - 0.5 * (pivots[v] * scale) * scale)
            rows[v] = [part * scale for part in rows[v]]
        n_a = size // LANES - home
        for v in range(4):
            for g in range(home + 1):
                b_ref[lo + 8 * v : lo + 8 * v + 8, g * LANES : (g + 1) * LANES] = rows[v][n_a + g]
        if lo + block == size:
            break
        whole = jnp.concatenate([jnp.concatenate(parts, axis=1) for parts in rows], axis=0)
        turned = whole[:, : n_a * LANES].T
        start = lo + block
        cuts = [start, start + block] + ([size] if start + block < size else [])
        for top, end in zip(cuts[:-1], cuts[1:]):
            first = home * LANES
            change = jnp.dot(turned[top - first : end - first], whole, precision=highest, preferred_element_type=f32)
            a_ref[top:end, first:] = a_ref[top:end, first:] - change[:, : n_a * LANES]
            b_ref[top:end, : (home + 1) * LANES] = b_ref[top:end, : (home + 1) * LANES] - change[:, n_a * LANES :]


def finish_kernel(gram_ref, root_ref, panel_ref, out_ref, a_ref, b_ref, w_ref, held_ref, sem):
    size = gram_ref.shape[0]
    width = out_ref.shape[1]

    @pl.when(pl.program_id(0) == 0)
    def _():
        fetch = pltpu.make_async_copy(panel_ref, held_ref, sem)
        fetch.start()
        a_ref[...] = gram_ref[...]
        b_ref[...] = (
            lax.broadcasted_iota(jnp.int32, (size, size), 0) == lax.broadcasted_iota(jnp.int32, (size, size), 1)
        ).astype(f32)
        factor_inverse(a_ref, b_ref)
        total = gram_ref[size - 1 : size, 0:1]
        inverse = b_ref[...] * jnp.sqrt(total)
        high, low = split_two(inverse)
        w_ref[:, :size] = high
        w_ref[:, size : 2 * size] = high
        w_ref[:, 2 * size :] = low
        fetch.wait()

    span = pl.ds(pl.multiple_of(pl.program_id(0) * width, width), width)
    high, low = split_two(held_ref[:, span] * root_ref[...])
    out_ref[...] = jnp.dot(w_ref[...], jnp.concatenate([high, low, high], axis=0), preferred_element_type=f32)


def finish(gram, root_weight, panel):
    columns, rows = panel.shape
    width = 2048
    return pl.pallas_call(
        finish_kernel,
        grid=(rows // width,),
        in_specs=[
            pl.BlockSpec((columns, columns), lambda i: (0, 0)),
            pl.BlockSpec((1, width), lambda i: (0, i)),
            pl.BlockSpec(memory_space=pl.ANY),
        ],
        out_specs=pl.BlockSpec((columns, width), lambda i: (0, i)),
        out_shape=jax.ShapeDtypeStruct((columns, rows), f32),
        scratch_shapes=[
            pltpu.VMEM((columns, columns), f32),
            pltpu.VMEM((columns, columns), f32),
            pltpu.VMEM((columns, 3 * columns), bf16),
            pltpu.VMEM((columns, rows), f32),
            pltpu.SemaphoreType.DMA,
        ],
        compiler_params=pltpu.CompilerParams(vmem_limit_bytes=48 * 1024 * 1024),
        name="factor_and_apply",
    )(gram, root_weight, pltpu.with_memory_space_constraint(panel, pltpu.HBM))


def on_device(panel, logits, signs, samples, counts):
    columns, rows_dev = panel.shape
    shards = 128
    total_rows = rows_dev * shards
    packed, root_weight = pack(panel, logits[None, :], signs[None, :], samples)
    arrived = lax.all_to_all(
        packed.reshape(shards, 65, 1, LANES), AXES, split_axis=0, concat_axis=0, tiled=True
    ).reshape(shards * 65, LANES)

    zero = jnp.minimum(counts[0], 0)
    m_hi, m_lo = rounded_parts(middle_table(zero))
    middle = jnp.concatenate([m_hi, m_lo], axis=2)

    picked = transform(arrived, middle, total_rows)
    mine = lax.all_to_all(picked, AXES, split_axis=0, concat_axis=0, tiled=True).reshape(columns, LANES)
    live = jnp.arange(LANES, dtype=jnp.int32)[None, :] < counts[0]
    sketch = jnp.where(live, mine * (1.0 / math.sqrt(total_rows)), 0.0)
    gram_part = jnp.dot(sketch, sketch.T, precision=highest)
    corner = (jnp.arange(columns)[:, None] == columns - 1) & (jnp.arange(columns)[None, :] == 0)
    gram_part = jnp.where(corner, counts[0].astype(f32), gram_part)
    lines = columns // shards
    strips = lax.all_to_all(
        gram_part.reshape(shards, lines, columns), AXES, split_axis=0, concat_axis=0, tiled=True
    ).sum(0)
    gram = lax.all_to_all(
        jnp.broadcast_to(strips[None], (shards, lines, columns)), AXES, split_axis=0, concat_axis=0, tiled=True
    ).reshape(columns, columns)
    return finish(gram, root_weight, panel)


def solution(mesh):
    placed = (
        P(None, AXES),
        P(AXES),
        P(AXES),
        P(AXES, None),
        P(AXES),
    )
    return jax.shard_map(on_device, mesh=mesh, in_specs=placed, out_specs=P(None, AXES), check_vma=False)
```

```python
import functools
import math

import jax
import jax.numpy as jnp
from jax import lax
from jax.experimental import pallas as pl
from jax.experimental.pallas import tpu as pltpu
from jax.sharding import PartitionSpec as P

AXES = ("row", "blk")
LANES = 128
highest = lax.Precision.HIGHEST
f32 = jnp.float32
bf16 = jnp.bfloat16


def split_two(value):
    high = value.astype(bf16)
    low = (value - high.astype(f32)).astype(bf16)
    return high, low


def rounded_parts(value):
    high = lax.reduce_precision(value, 8, 7)
    return high.astype(bf16), (value - high).astype(bf16)


def cos_turns(numerator, length):
    return jnp.cos((2.0 * math.pi / length) * (numerator % length).astype(f32))


def swap_eight(tiles):
    tiles = list(tiles)
    line = lax.broadcasted_iota(jnp.int32, tiles[0].shape, 0)
    for d in (4, 2, 1):
        low = (line & d) == 0
        for i in range(8):
            if i & d == 0:
                first, second = tiles[i], tiles[i + d]
                tiles[i] = jnp.where(low, first, pltpu.roll(second, d, 0))
                tiles[i + d] = jnp.where(low, pltpu.roll(first, 8 - d, 0), second)
    return tiles


def pack_kernel(panel_ref, logits_ref, signs_ref, samples_ref, out_ref, root_ref, scale_ref, rider_ref):
    lines = panel_ref.shape[0]
    groups = panel_ref.shape[1] // LANES
    slots = samples_ref.shape[1]

    @pl.when(pl.program_id(0) == 0)
    def _():
        probability = 1.0 / (1.0 + jnp.exp(-logits_ref[...]))
        root = jnp.sqrt(probability * (1.0 - probability))
        root_ref[...] = root
        scale_ref[...] = root * signs_ref[...].astype(f32)
        rider_ref[...] = jnp.zeros_like(rider_ref)
        rider_ref[:, :slots] = jnp.broadcast_to(samples_ref[...].astype(f32), (8, slots))

    for top in range(0, lines, 8):
        for g in range(0, groups, 8):
            spans = [slice((g + i) * LANES, (g + i + 1) * LANES) for i in range(8)]
            tiles = swap_eight([panel_ref[top : top + 8, span] * scale_ref[:, span] for span in spans])
            for i in range(8):
                line = top + i
                row = (line // 2) * (2 * groups + 1) + (line % 2) * groups + g
                out_ref[row : row + 8, :] = tiles[i]
    for q in range(lines // 2):
        row = (q + 1) * (2 * groups + 1) - 1
        out_ref[row : row + 1, :] = rider_ref[:1]


def pack(panel, logits, signs, samples):
    columns, rows = panel.shape
    groups = rows // LANES
    step = 128
    whole = pl.BlockSpec((1, rows), lambda i: (0, 0))
    return pl.pallas_call(
        pack_kernel,
        grid=(columns // step,),
        in_specs=[
            pl.BlockSpec((step, rows), lambda i: (i, 0)),
            whole,
            whole,
            pl.BlockSpec(samples.shape, lambda i: (0, 0)),
        ],
        out_specs=[pl.BlockSpec((step // 2 * (2 * groups + 1), LANES), lambda i: (i, 0)), whole],
        out_shape=[
            jax.ShapeDtypeStruct((columns // 2 * (2 * groups + 1), LANES), f32),
            jax.ShapeDtypeStruct((1, rows), f32),
        ],
        scratch_shapes=[pltpu.VMEM((1, rows), f32), pltpu.VMEM((8, LANES), f32)],
        name="pack_columns",
    )(panel, logits, signs, samples)


def unit_circle(step, log_length):
    quarter = log_length - 2
    turn = (step + (1 << (quarter - 1))) >> quarter
    x = (step - (turn << quarter)).astype(f32) * (2.0 * math.pi / (1 << log_length))
    x2 = x * x
    sine = x + x * x2 * (-1 / 6 + x2 * (1 / 120 + x2 * (-1 / 5040 + x2 * (1 / 362880))))
    cosine = 1.0 + x2 * (-0.5 + x2 * (1 / 24 + x2 * (-1 / 720 + x2 * (1 / 40320))))
    odd = (turn & 1) == 1
    a, b = jnp.where(odd, sine, cosine), jnp.where(odd, cosine, sine)
    return jnp.where(((turn + 1) & 2) != 0, -a, a), jnp.where((turn & 2) != 0, -b, b)


def sample_phases(frequency, log_length):
    line = lax.broadcasted_iota(jnp.int32, (8, LANES), 0)
    last = (1 << log_length) - 1
    eighth = 1 << (log_length - 3)
    c2, s2 = unit_circle((frequency * line - eighth) & last, log_length)
    c2, s2 = c2 * math.sqrt(2.0), s2 * math.sqrt(2.0)
    res, ims = [], []
    for half in range(2):
        c8, s8 = unit_circle((frequency * (8 * line + 64 * half)) & last, log_length)
        for a in range(8):
            c1, s1 = c8[a : a + 1], s8[a : a + 1]
            res.append(c1 * c2 - s1 * s2)
            ims.append(c1 * s2 + s1 * c2)
    return jnp.concatenate(res + ims, axis=0)


def middle_table(zero):
    shape = (64, 2, 2, 32, 2, 32)
    p, cls, part, s1, c, ib = (lax.broadcasted_iota(jnp.int32, shape, k) for k in range(6))
    p = p + zero
    e = jnp.where(cls == 0, p, jnp.where(p == 0, 64, 128 - p))
    angle = ib * (e + 128 * s1)
    quarters = jnp.where(cls == 0, part + c, jnp.where(p == 0, part, jnp.where(c == 0, part, 3 * (1 - part))))
    value = cos_turns(angle + 1024 * quarters, 4096)
    value = jnp.where((p == 0) & (c != cls), 0.0, value)
    return value.reshape(64, 128, 64)


def times(value, turn):
    re, im = value
    turn = turn % 1.0
    if turn == 0.0:
        return re, im
    c, s = math.cos(2.0 * math.pi * turn), math.sin(2.0 * math.pi * turn)
    if turn == 0.25:
        return (None if im is None else -im), re
    if turn == 0.5:
        return -re, (None if im is None else -im)
    if im is None:
        return re * c, re * s
    if turn in (0.125, 0.375, 0.625, 0.875):
        root = math.sqrt(0.5)
        plus, minus = (re + im) * root, (re - im) * root
        if turn == 0.125:
            return minus, plus
        if turn == 0.375:
            return -plus, minus
        if turn == 0.625:
            return -minus, -plus
        return plus, -minus
    return re * c - im * s, re * s + im * c


def add(a, b):
    return tuple(y if x is None else (x if y is None else x + y) for x, y in zip(a, b))


def sub(a, b):
    return tuple((None if y is None else -y) if x is None else (x if y is None else x - y) for x, y in zip(a, b))


def small_dft(values):
    length = len(values)
    if length == 1:
        return values
    even, odd = small_dft(values[0::2]), small_dft(values[1::2])
    turned = [times(odd[k], k / length) for k in range(length // 2)]
    return [add(even[k], turned[k]) for k in range(length // 2)] + [sub(even[k], turned[k]) for k in range(length // 2)]


def block_dft(data_ref, part, y_ref, top):
    inner = [small_dft([(data_ref[(16 * n + m) * 65 + part : (16 * n + m) * 65 + part + 8], None) for n in range(8)]) for m in range(16)]
    for r in range(5):
        outs = small_dft([times(inner[m][r], m * r / 128) for m in range(16)])
        for f in range(16):
            e = r + 8 * f
            re, im = outs[f]
            if e in (0, 64):
                y_ref[e // 64, pl.ds(top, 8), :] = re
            elif e < 64:
                y_ref[2 * e, pl.ds(top, 8), :] = re
                y_ref[2 * e + 1, pl.ds(top, 8), :] = im
            elif r in (1, 2, 3):
                y_ref[2 * (128 - e), pl.ds(top, 8), :] = re
                y_ref[2 * (128 - e) + 1, pl.ds(top, 8), :] = -im


DATA_STEPS = 1


def transform_kernel(data_ref, middle_ref, out_ref, y_ref, *, log_length):
    step = pl.program_id(0)
    pairs = middle_ref.shape[0]

    @pl.when(step < DATA_STEPS)
    def _():
        for part in range(0, 64, 8):
            block_dft(data_ref, part, y_ref, part)

    @pl.when(step >= DATA_STEPS)
    def _():
        products = []
        for q in range(pairs):
            pair = (step - DATA_STEPS) * pairs + q
            cosines = y_ref[2 * pair]
            sines = y_ref[2 * pair + 1]
            stack = jnp.concatenate(
                [
                    jnp.concatenate([cosines[:32], cosines[32:]], axis=1),
                    jnp.concatenate([sines[:32], sines[32:]], axis=1),
                ],
                axis=0,
            )
            hi, lo = split_two(stack)
            mid = middle_ref[q]
            z = jnp.dot(
                jnp.concatenate([mid, mid[:, :64]], axis=1),
                jnp.concatenate([hi, hi, lo], axis=0),
                preferred_element_type=f32,
            )
            products.append(z)
        for q in range(pairs):
            z = products[q]
            pair = (step - DATA_STEPS) * pairs + q
            for cls in range(2):
                zr = z[cls * 64 : cls * 64 + 32]
                zi = z[cls * 64 + 32 : cls * 64 + 64]
                left = jnp.concatenate(
                    [
                        jnp.concatenate([zr[:, :128], zi[:, :128]], axis=1),
                        jnp.concatenate([zr[:, 128:], zi[:, 128:]], axis=1),
                    ],
                    axis=0,
                )
                hi, lo = split_two(left)
                if cls == 0:
                    e = pair
                else:
                    e = jnp.where(pair == 0, 64, 128 - pair)
                offset = jnp.broadcast_to(data_ref[pl.ds(e * 65 + 64, 1), :].astype(jnp.int32), (8, LANES))
                t_hi, t_lo = split_two(sample_phases(offset * 128 + e, log_length))
                both = jnp.dot(
                    jnp.concatenate([hi, lo], axis=0),
                    jnp.concatenate([t_hi, t_lo], axis=1),
                    preferred_element_type=f32,
                )
                res = both[:64, :LANES] + both[64:, :LANES] + both[:64, LANES:]
                wanted = jnp.concatenate([offset & 31] * 4, axis=0)
                mask = lax.broadcasted_iota(jnp.int32, (32, LANES), 0) == wanted
                first = jnp.sum(jnp.where(mask, res[:32], 0.0), axis=0, keepdims=True)
                second = jnp.sum(jnp.where(mask, res[32:], 0.0), axis=0, keepdims=True)
                out_ref[e] = jnp.concatenate([first, second], axis=0)


def transform(data, middle, total_rows):
    pairs = 8
    return pl.pallas_call(
        functools.partial(transform_kernel, log_length=total_rows.bit_length() - 1),
        grid=(DATA_STEPS + 64 // pairs,),
        in_specs=[
            pl.BlockSpec(data.shape, lambda i: (0, 0)),
            pl.BlockSpec((pairs, 128, 128), lambda i: (jnp.maximum(i - DATA_STEPS, 0), 0, 0)),
        ],
        out_specs=pl.BlockSpec((128, 2, LANES), lambda i: (0, 0, 0)),
        out_shape=jax.ShapeDtypeStruct((128, 2, LANES), f32),
        scratch_shapes=[pltpu.VMEM((128, 64, LANES), f32)],
        compiler_params=pltpu.CompilerParams(vmem_limit_bytes=48 * 1024 * 1024),
        name="sampled_transform",
    )(data, middle)


def factor_inverse(a_ref, b_ref):
    size = a_ref.shape[0]
    block = 64
    line = lax.broadcasted_iota(jnp.int32, (8, LANES), 0)
    spread = lambda row: jnp.broadcast_to(row, (8, LANES))
    for lo in range(0, size, block):
        home = lo // LANES
        off = lo % LANES
        spots = [(a_ref, g) for g in range(home, size // LANES)] + [(b_ref, g) for g in range(home + 1)]
        rows = [[ref[lo + 8 * v : lo + 8 * v + 8, g * LANES : (g + 1) * LANES] for ref, g in spots] for v in range(block // 8)]
        pivots = []
        for t in range(block // 8):
            col = [
                {v: jnp.broadcast_to(rows[v][0][:, off + 8 * t + j : off + 8 * t + j + 1], (8, LANES)) for v in range(t, block // 8)}
                for j in range(8)
            ]
            diag = jnp.ones((8, LANES), f32)
            for j in range(8):
                pivot = spread(col[j][t][j : j + 1])
                inverse = 1.0 / pivot
                diag = jnp.where(line == j, pivot, diag)
                mult = {v: col[j][v] * inverse for v in range(t, block // 8)}
                mult[t] = jnp.where(line > j, mult[t], 0.0)
                for n in range(j + 1, 8):
                    across = spread(col[j][t][n : n + 1])
                    for v in range(t, block // 8):
                        col[n][v] = col[n][v] - mult[v] * across
                for g in range(len(spots)):
                    across = spread(rows[t][g][j : j + 1])
                    for v in range(t, block // 8):
                        rows[v][g] = rows[v][g] - mult[v] * across
            pivots.append(diag)
        for v in range(block // 8):
            scale = lax.rsqrt(pivots[v])
            scale = scale * (1.5 - 0.5 * (pivots[v] * scale) * scale)
            rows[v] = [part * scale for part in rows[v]]
        n_a = size // LANES - home
        for v in range(block // 8):
            for g in range(home + 1):
                b_ref[lo + 8 * v : lo + 8 * v + 8, g * LANES : (g + 1) * LANES] = rows[v][n_a + g]
        if lo + block == size:
            break
        whole = jnp.concatenate([jnp.concatenate(parts, axis=1) for parts in rows], axis=0)
        turned = whole[:, : n_a * LANES].T
        start = lo + block
        cuts = [start, start + block] + ([size] if start + block < size else [])
        for top, end in zip(cuts[:-1], cuts[1:]):
            first = home * LANES
            change = jnp.dot(turned[top - first : end - first], whole, precision=highest, preferred_element_type=f32)
            a_ref[top:end, first:] = a_ref[top:end, first:] - change[:, : n_a * LANES]
            b_ref[top:end, : (home + 1) * LANES] = b_ref[top:end, : (home + 1) * LANES] - change[:, n_a * LANES :]


def finish_kernel(gram_ref, high_ref, low_ref, out_ref, a_ref, b_ref, w_ref, held_ref, sems):
    size = gram_ref.shape[0]
    width = out_ref.shape[1]

    @pl.when(pl.program_id(0) == 0)
    def _():
        fetches = [
            pltpu.make_async_copy(source, held_ref.at[k], sems.at[k]) for k, source in enumerate((high_ref, low_ref))
        ]
        for fetch in fetches:
            fetch.start()
        a_ref[...] = gram_ref[...]
        b_ref[...] = (
            lax.broadcasted_iota(jnp.int32, (size, size), 0) == lax.broadcasted_iota(jnp.int32, (size, size), 1)
        ).astype(f32)
        factor_inverse(a_ref, b_ref)
        total = gram_ref[size - 1 : size, 0:1]
        inverse = b_ref[...] * jnp.sqrt(total)
        high, low = split_two(inverse)
        w_ref[:, :size] = high
        w_ref[:, size : 2 * size] = high
        w_ref[:, 2 * size :] = low
        for fetch in fetches:
            fetch.wait()

    span = pl.ds(pl.multiple_of(pl.program_id(0) * width, width), width)
    high, low = held_ref[0, :, span], held_ref[1, :, span]
    out_ref[...] = jnp.dot(w_ref[...], jnp.concatenate([high, low, high], axis=0), preferred_element_type=f32)


def finish(gram, high, low):
    columns, rows = high.shape
    width = 2048
    return pl.pallas_call(
        finish_kernel,
        grid=(rows // width,),
        in_specs=[
            pl.BlockSpec((columns, columns), lambda i: (0, 0)),
            pl.BlockSpec(memory_space=pl.ANY),
            pl.BlockSpec(memory_space=pl.ANY),
        ],
        out_specs=pl.BlockSpec((columns, width), lambda i: (0, i)),
        out_shape=jax.ShapeDtypeStruct((columns, rows), f32),
        scratch_shapes=[
            pltpu.VMEM((columns, columns), f32),
            pltpu.VMEM((columns, columns), f32),
            pltpu.VMEM((columns, 3 * columns), bf16),
            pltpu.VMEM((2, columns, rows), bf16),
            pltpu.SemaphoreType.DMA((2,)),
        ],
        compiler_params=pltpu.CompilerParams(vmem_limit_bytes=48 * 1024 * 1024),
        name="factor_and_apply",
    )(gram, *(pltpu.with_memory_space_constraint(part, pltpu.HBM) for part in (high, low)))


def on_device(panel, logits, signs, samples, counts):
    columns, rows_dev = panel.shape
    shards = 128
    total_rows = rows_dev * shards
    packed, root_weight = pack(panel, logits[None, :], signs[None, :], samples)
    arrived = lax.all_to_all(
        packed.reshape(shards, 65, 1, LANES), AXES, split_axis=0, concat_axis=0, tiled=True
    ).reshape(shards * 65, LANES)

    zero = jnp.minimum(counts[0], 0)
    m_hi, m_lo = rounded_parts(middle_table(zero))
    middle = jnp.concatenate([m_hi, m_lo], axis=2)

    picked = transform(arrived, middle, total_rows)
    mine = lax.all_to_all(picked, AXES, split_axis=0, concat_axis=0, tiled=True).reshape(columns, LANES)
    live = jnp.arange(LANES, dtype=jnp.int32)[None, :] < counts[0]
    sketch = jnp.where(live, mine * (1.0 / math.sqrt(total_rows)), 0.0)
    gram_part = jnp.dot(sketch, sketch.T, precision=highest)
    corner = (jnp.arange(columns)[:, None] == columns - 1) & (jnp.arange(columns)[None, :] == 0)
    gram_part = jnp.where(corner, counts[0].astype(f32), gram_part)
    lines = columns // shards
    strips = lax.all_to_all(
        gram_part.reshape(shards, lines, columns), AXES, split_axis=0, concat_axis=0, tiled=True
    ).sum(0)
    gram = lax.all_to_all(
        jnp.broadcast_to(strips[None], (shards, lines, columns)), AXES, split_axis=0, concat_axis=0, tiled=True
    ).reshape(columns, columns)
    return finish(gram, *rounded_parts(panel * root_weight))


def solution(mesh):
    placed = (
        P(None, AXES),
        P(AXES),
        P(AXES),
        P(AXES, None),
        P(AXES),
    )
    return jax.shard_map(on_device, mesh=mesh, in_specs=placed, out_specs=P(None, AXES), check_vma=False)
```
